32 devices in a mesh: dp: 8 (over y, x, core), tensor: 4 (over z).
Axes of the slice: x: 2, y: 2, z: 4, core: 2. Of those that a mesh axis runs over, the one named last changes fastest.
Arguments:
- block_input: bfloat16 [8192, 1024], P(('dp', 'tensor')), may hold values from -24 to 24
- lengths: int32 [8], P('dp'), may hold values from 128 to 1024, as said below
- query_weight: bfloat16 [1024, 1024], P('dp', 'tensor'), may hold values from -0.1875 to 0.1875
- key_weight: bfloat16 [1024, 1024], P('dp', 'tensor'), may hold values from -0.1875 to 0.1875
- value_weight: bfloat16 [1024, 1024], P('dp', 'tensor'), may hold values from -0.1875 to 0.1875
- query_bias: bfloat16 [1024], P(('tensor', 'dp')), may hold values from -4 to 4
- value_bias: bfloat16 [1024], P(('tensor', 'dp')), may hold values from -4 to 4
- output_weight: bfloat16 [1024, 1024], P('tensor', 'dp'), may hold values from -0.75 to 0.75
- output_bias: float32 [1024], P(('dp', 'tensor')), may hold values from -4 to 4
- first_gain: float32 [1024], P(('dp', 'tensor')), may hold values from 0.1 to 1.9
- first_shift: float32 [1024], P(('dp', 'tensor')), may hold values from -3 to 3
- inner_weight: bfloat16 [1024, 4096], P('dp', 'tensor'), may hold values from -0.1875 to 0.1875
- inner_bias: bfloat16 [4096], P(('tensor', 'dp')), may hold values from -3 to 3
- outer_weight: bfloat16 [4096, 1024], P('tensor', 'dp'), may hold values from -0.09375 to 0.09375
- outer_bias: float32 [1024], P(('dp', 'tensor')), may hold values from -4 to 4
- second_gain: float32 [1024], P(('dp', 'tensor')), may hold values from 0.1 to 1.9
- second_shift: float32 [1024], P(('dp', 'tensor')), may hold values from -3 to 3
- cotangent: bfloat16 [8192, 1024], P(('dp', 'tensor')), may hold values from -6 to 6
Outputs:
- block_output: bfloat16 [8192, 1024], P(('dp', 'tensor'))
- input_grad: float32 [8192, 1024], P(('dp', 'tensor'))
- query_weight_grad: float32 [1024, 1024], P('dp', 'tensor')
- key_weight_grad: float32 [1024, 1024], P('dp', 'tensor')
- value_weight_grad: float32 [1024, 1024], P('dp', 'tensor')
- query_bias_grad: float32 [1024], P(('tensor', 'dp'))
- value_bias_grad: float32 [1024], P(('tensor', 'dp'))
- output_weight_grad: float32 [1024, 1024], P('tensor', 'dp')
- output_bias_grad: float32 [1024], P(('dp', 'tensor'))
- first_gain_grad: float32 [1024], P(('dp', 'tensor'))
- first_shift_grad: float32 [1024], P(('dp', 'tensor'))
- inner_weight_grad: float32 [1024, 4096], P('dp', 'tensor')
- inner_bias_grad: float32 [4096], P(('tensor', 'dp'))
- outer_weight_grad: float32 [4096, 1024], P('tensor', 'dp')
- outer_bias_grad: float32 [1024], P(('dp', 'tensor'))
- second_gain_grad: float32 [1024], P(('dp', 'tensor'))
- second_shift_grad: float32 [1024], P(('dp', 'tensor'))
The draws below stay inside these ranges and needn't reach their ends.
Inputs may be any that keep to these rules, and one draw needn't show every extreme that they name: lengths[s] tokens at the start of sequence s are valid keys; one sequence is full and one has the fewest.
All inputs are finite; a program needn't handle non-finite values.
Results may differ from the reference program's by a relative error of at most 0.009.
The reference program's roundings to bfloat16 on the way count: a program that leaves them out, or rounds other values in their place, can miss the bound.
Values may be sent and summed in bfloat16 or wider, within the bound.
A program may use at most 128 MiB of HBM per device.

```python
import math
import jax
import jax.numpy as jnp
from jax import lax

D = 1024
HEADS = 16
HEAD_DIM = 64
FF = 4096
SEQ_LEN = 1024
SEQUENCES = 8
TOKENS = 8192


def draw_block_input(key, part):
    key_base, key_scale = jax.random.split(key)
    base_draw = jnp.clip(jax.random.normal(key_base, (TOKENS, D), jnp.float32), -6.0, 6.0)
    top_log = math.log(3.0)
    row_scale = jnp.exp(jax.random.uniform(key_scale, (TOKENS, 1), jnp.float32, 0.0, top_log))
    return (base_draw * row_scale).astype(jnp.bfloat16)


def draw_lengths(key, part):
    key_len, key_pick = jax.random.split(key)
    drawn_len = jax.random.randint(key_len, (SEQUENCES,), SEQ_LEN // 8, SEQ_LEN + 1)
    picked = jax.random.permutation(key_pick, SEQUENCES)
    drawn_len = drawn_len.at[picked[0]].set(SEQ_LEN)
    drawn_len = drawn_len.at[picked[1]].set(SEQ_LEN // 8)
    return drawn_len.astype(jnp.int32)


def raised(result, stream_key, source, target, shards_of, factor):
    def block_of(position):
        return (jnp.arange(result.shape[position]) // (result.shape[position] // shards_of)).reshape((-1,) + (1,) * (result.ndim - 1 - position))

    one_side = jax.random.permutation(stream_key, shards_of)[block_of(target)]
    far = (block_of(target) + shards_of // 2) % shards_of
    return jnp.where((block_of(source) == one_side) | (block_of(source) == far), factor * result, result)


def shard_levels(rng, extent, cuts, smallest, top_value):
    factor_of = 1.0
    for dim, shards_of in cuts:
        heights = jax.random.uniform(jax.random.fold_in(jax.random.fold_in(rng, 6), dim), (shards_of,), jnp.float32, smallest / len(cuts), top_value / len(cuts))
        factor_of = factor_of * jnp.repeat(jnp.exp(heights), extent[dim] // shards_of).reshape((-1,) + (1,) * (len(extent) - 1 - dim))
    return factor_of


def scatter_about(key, shape, width, limit, cuts=(), dtype=jnp.bfloat16):
    result = width * jax.random.normal(key, shape, jnp.float32)
    if cuts:
        result = result * shard_levels(key, shape, cuts, -0.22, 0.18)
    return jnp.clip(result, -limit, limit).astype(dtype)


def gaussian_with(key, shape, deviation, bound, cuts, heavy, held_as=jnp.bfloat16):
    values = deviation * jax.random.normal(key, shape, jnp.float32)
    if cuts:
        values = values * shard_levels(key, shape, cuts, -0.22, 0.18)
    return jnp.clip(raised(values, jax.random.fold_in(key, 3), *heavy), -bound, bound).astype(held_as)


def setup_inputs(seed: int = 0) -> dict:
    arg_keys = jax.random.split(jax.random.key(seed), 19)
    block_input = draw_block_input(jax.random.fold_in(arg_keys[18], 71), 0)
    lengths = draw_lengths(jax.random.fold_in(arg_keys[18], 71), 0)
    query_weight = scatter_about(arg_keys[2], (D, D), D ** -0.5, 0.1875, ((0, 8), (1, 4)))
    key_weight = scatter_about(arg_keys[3], (D, D), D ** -0.5, 0.1875, ((0, 8), (1, 4)))
    value_weight = scatter_about(arg_keys[4], (D, D), D ** -0.5, 0.1875, ((0, 8), (1, 4)))
    query_bias = scatter_about(arg_keys[5], (D,), 1.0, 4.0, ((0, 32),))
    value_bias = scatter_about(arg_keys[6], (D,), 1.0, 4.0, ((0, 32),))
    output_weight = scatter_about(arg_keys[7], (D, D), (D // 16) ** -0.5, 0.75, ((0, 4), (1, 8)))
    output_bias = scatter_about(arg_keys[8], (D,), 1.0, 4.0, ((0, 32),), jnp.float32)
    first_gain = jnp.clip(1.0 + 0.18 * jax.random.normal(arg_keys[9], (D,), jnp.float32), 0.1, 1.9)
    first_shift = scatter_about(arg_keys[10], (D,), 0.5, 3.0, ((0, 32),), jnp.float32)
    inner_weight = scatter_about(arg_keys[11], (D, FF), D ** -0.5, 0.1875, ((0, 8), (1, 4)))
    inner_bias = scatter_about(arg_keys[12], (FF,), 0.5, 3.0, ((0, 32),))
    outer_weight = scatter_about(arg_keys[13], (FF, D), FF ** -0.5, 0.09375, ((0, 4), (1, 8)))
    outer_bias = scatter_about(arg_keys[14], (D,), 1.0, 4.0, ((0, 32),), jnp.float32)
    second_gain = jnp.clip(1.0 + 0.18 * jax.random.normal(arg_keys[15], (D,), jnp.float32), 0.1, 1.9)
    second_shift = scatter_about(arg_keys[16], (D,), 0.5, 3.0, ((0, 32),), jnp.float32)
    cotangent = gaussian_with(arg_keys[17], (TOKENS, D), 1.0, 6.0, ((0, 32),), (0, 1, 32, 2.75))
    return {"block_input": block_input, "lengths": lengths, "query_weight": query_weight, "key_weight": key_weight, "value_weight": value_weight, "query_bias": query_bias, "value_bias": value_bias, "output_weight": output_weight, "output_bias": output_bias, "first_gain": first_gain, "first_shift": first_shift, "inner_weight": inner_weight, "inner_bias": inner_bias, "outer_weight": outer_weight, "outer_bias": outer_bias, "second_gain": second_gain, "second_shift": second_shift, "cotangent": cotangent}


inv_root2 = 0.7071067811865476
inv_root2pi = 0.3989422804014327
norm_eps = 1e-06

def gelu_cdf(values):
    return 0.5 * (1.0 + jax.scipy.special.erf(values * inv_root2))

def row_norm(resid_rows, norm_gain, norm_shift):
    center = resid_rows - lax.optimization_barrier(jnp.mean(resid_rows, axis=-1, keepdims=True))
    inverse = lax.rsqrt(lax.optimization_barrier(jnp.mean(center * center, axis=-1, keepdims=True)) + norm_eps)
    return center * inverse * norm_gain + norm_shift

def norm_back(resid_rows, norm_gain, upstream):
    center = resid_rows - lax.optimization_barrier(jnp.mean(resid_rows, axis=-1, keepdims=True))
    inverse = lax.rsqrt(lax.optimization_barrier(jnp.mean(center * center, axis=-1, keepdims=True)) + norm_eps)
    normed = center * inverse
    scaled_up = upstream * norm_gain
    d_resid = inverse * (scaled_up - lax.optimization_barrier(jnp.mean(scaled_up, axis=-1, keepdims=True)) - normed * lax.optimization_barrier(jnp.mean(scaled_up * normed, axis=-1, keepdims=True)))
    return (d_resid, lax.optimization_barrier(jnp.sum(upstream * normed, axis=0)), lax.optimization_barrier(jnp.sum(upstream, axis=0)))

def round_keep(values):
    return lax.optimization_barrier(values.astype(jnp.bfloat16))

def dense(left, right):
    return jnp.dot(left, right, preferred_element_type=jnp.float32)

def split_heads(matrix):
    return matrix.reshape(SEQ_LEN, HEADS, HEAD_DIM).astype(jnp.float32)

def reference(block_input, lengths, query_weight, key_weight, value_weight, query_bias, value_bias, output_weight, output_bias, first_gain, first_shift, inner_weight, inner_bias, outer_weight, outer_bias, second_gain, second_shift, cotangent):
    scale_qk = HEAD_DIM ** (-0.5)

    def one_sequence(totals, pieces):
        seq_rows, upstream, length = pieces
        q_rows = round_keep(dense(seq_rows, query_weight) + query_bias.astype(jnp.float32))
        k_rows = round_keep(dense(seq_rows, key_weight))
        v_rows = round_keep(dense(seq_rows, value_weight) + value_bias.astype(jnp.float32))
        q_heads = split_heads(q_rows)
        k_heads = split_heads(k_rows)
        v_heads = split_heads(v_rows)
        key_valid = jnp.arange(SEQ_LEN) < length
        scores = jnp.einsum('qhd,khd->hqk', q_heads, k_heads) * scale_qk
        scores = jnp.where(key_valid[None, None, :], scores, -jnp.inf)
        row_top = lax.optimization_barrier(jnp.max(scores, axis=-1, keepdims=True))
        log_total = row_top + jnp.log(lax.optimization_barrier(jnp.sum(jnp.exp(scores - row_top), axis=-1, keepdims=True)))
        attn_probs = jnp.exp(scores - log_total)
        probs_b = round_keep(attn_probs).astype(jnp.float32)
        context = round_keep(jnp.einsum('hqk,khd->qhd', probs_b, v_heads).reshape(SEQ_LEN, D))
        resid_one = seq_rows.astype(jnp.float32) + dense(context, output_weight) + output_bias
        middle = row_norm(resid_one, first_gain, first_shift)
        middle_b = round_keep(middle)
        pre_act = dense(middle_b, inner_weight) + inner_bias.astype(jnp.float32)
        hidden_b = round_keep(pre_act * gelu_cdf(pre_act))
        resid_two = middle + dense(hidden_b, outer_weight) + outer_bias
        block_out = row_norm(resid_two, second_gain, second_shift).astype(jnp.bfloat16)
        d_resid2, gain2_grad, shift2_grad = norm_back(resid_two, second_gain, upstream.astype(jnp.float32))
        d_ffn = round_keep(d_resid2)
        outer_grad = dense(hidden_b.T, d_ffn)
        gelu_slope = gelu_cdf(pre_act) + pre_act * inv_root2pi * jnp.exp(-0.5 * pre_act * pre_act)
        d_pre = dense(d_ffn, outer_weight.T) * gelu_slope
        d_pre_b = round_keep(d_pre)
        inner_grad = dense(middle_b.T, d_pre_b)
        d_middle = dense(d_pre_b, inner_weight.T) + d_resid2
        d_resid1, gain1_grad, shift1_grad = norm_back(resid_one, first_gain, d_middle)
        d_attn = round_keep(d_resid1)
        output_grad = dense(context.T, d_attn)
        d_context = round_keep(dense(d_attn, output_weight.T))
        d_ctx_heads = split_heads(d_context)
        d_probs = jnp.einsum('qhd,khd->hqk', d_ctx_heads, v_heads)
        row_inner = lax.optimization_barrier(jnp.sum(attn_probs * d_probs, axis=-1, keepdims=True))
        d_scores = round_keep(attn_probs * (d_probs - row_inner) * scale_qk).astype(jnp.float32)
        d_query = jnp.einsum('hqk,khd->qhd', d_scores, k_heads).reshape(SEQ_LEN, D)
        d_key = jnp.einsum('hqk,qhd->khd', d_scores, q_heads).reshape(SEQ_LEN, D)
        d_value = jnp.einsum('hqk,qhd->khd', probs_b, d_ctx_heads).reshape(SEQ_LEN, D)
        dq_b = round_keep(d_query)
        dk_b = round_keep(d_key)
        dv_b = round_keep(d_value)
        d_input = d_resid1 + dense(dq_b, query_weight.T) + dense(dk_b, key_weight.T) + dense(dv_b, value_weight.T)
        terms = (dense(seq_rows.T, dq_b), dense(seq_rows.T, dk_b), dense(seq_rows.T, dv_b), lax.optimization_barrier(jnp.sum(d_query, axis=0)), lax.optimization_barrier(jnp.sum(d_value, axis=0)), output_grad, lax.optimization_barrier(jnp.sum(d_resid1, axis=0)), gain1_grad, shift1_grad, inner_grad, lax.optimization_barrier(jnp.sum(d_pre, axis=0)), outer_grad, lax.optimization_barrier(jnp.sum(d_resid2, axis=0)), gain2_grad, shift2_grad)
        totals = jax.tree.map(lambda left, right: left + right, totals, terms)
        return (totals, (block_out, d_input))
    zero_totals = (jnp.zeros((D, D), jnp.float32), jnp.zeros((D, D), jnp.float32), jnp.zeros((D, D), jnp.float32), jnp.zeros((D,), jnp.float32), jnp.zeros((D,), jnp.float32), jnp.zeros((D, D), jnp.float32), jnp.zeros((D,), jnp.float32), jnp.zeros((D,), jnp.float32), jnp.zeros((D,), jnp.float32), jnp.zeros((D, FF), jnp.float32), jnp.zeros((FF,), jnp.float32), jnp.zeros((FF, D), jnp.float32), jnp.zeros((D,), jnp.float32), jnp.zeros((D,), jnp.float32), jnp.zeros((D,), jnp.float32))
    inputs = (block_input.reshape(SEQUENCES, SEQ_LEN, D), cotangent.reshape(SEQUENCES, SEQ_LEN, D), lengths)
    totals, (outputs, input_grads) = lax.scan(one_sequence, zero_totals, inputs)
    return (outputs.reshape(TOKENS, D), input_grads.reshape(TOKENS, D)) + totals
```

```python
import jax
import jax.numpy as jnp
from jax import lax
from jax.experimental import pallas as pl
from jax.experimental.pallas import tpu as pltpu
from jax.sharding import PartitionSpec as P

HEAD_DIM = 64


inv_root2 = 0.7071067811865476
inv_root2pi = 0.3989422804014327
norm_eps = 1e-06


def gelu_cdf(values):
    return 0.5 * (1.0 + jax.scipy.special.erf(values * inv_root2))


def row_norm(resid_rows, norm_gain, norm_shift):
    center = resid_rows - jnp.mean(resid_rows, axis=-1, keepdims=True)
    inverse = lax.rsqrt(jnp.mean(center * center, axis=-1, keepdims=True) + norm_eps)
    return center * inverse * norm_gain + norm_shift


def norm_back(resid_rows, norm_gain, upstream):
    center = resid_rows - jnp.mean(resid_rows, axis=-1, keepdims=True)
    inverse = lax.rsqrt(jnp.mean(center * center, axis=-1, keepdims=True) + norm_eps)
    normed = center * inverse
    scaled_up = upstream * norm_gain
    d_resid = inverse * (
        scaled_up
        - jnp.mean(scaled_up, axis=-1, keepdims=True)
        - normed * jnp.mean(scaled_up * normed, axis=-1, keepdims=True)
    )
    return (d_resid, jnp.sum(upstream * normed, axis=0), jnp.sum(upstream, axis=0))


def dense(left, right):
    return jnp.dot(left, right, preferred_element_type=jnp.float32)


def dense_tn(left, right):
    return lax.dot_general(
        left, right, (((0,), (0,)), ((), ())), preferred_element_type=jnp.float32
    )


def dense_nt(left, right):
    return lax.dot_general(
        left, right, (((1,), (1,)), ((), ())), preferred_element_type=jnp.float32
    )


def whole_rows(part_rows):
    return lax.all_gather(part_rows, "tensor", axis=0, tiled=True)


def share_rows(partial_value):
    partial_b = partial_value.astype(jnp.bfloat16)
    return lax.psum_scatter(partial_b, "tensor", scatter_dimension=0, tiled=True).astype(jnp.float32)


def share_grad(partial_value, axis):
    partial_b = partial_value.astype(jnp.bfloat16)
    return lax.psum_scatter(partial_b, "dp", scatter_dimension=axis, tiled=True).astype(jnp.float32)


def gather_vectors(vectors, biases):
    mesh_dp, mesh_tensor = lax.axis_size("dp"), lax.axis_size("tensor")
    parts = list(vectors) + [bias.astype(jnp.float32) for bias in biases]
    packed = jnp.concatenate(parts)[None, :]
    every = lax.all_gather(packed, ("dp", "tensor"), axis=0, tiled=True)
    full, start = [], 0
    for part in vectors:
        full.append(every[:, start : start + part.shape[0]].reshape(-1))
        start += part.shape[0]
    own = lax.dynamic_index_in_dim(
        every.reshape(mesh_dp, mesh_tensor, -1), lax.axis_index("tensor"), 1, keepdims=False
    )
    for part in biases:
        full.append(own[:, start : start + part.shape[0]].reshape(-1))
        start += part.shape[0]
    return full


def share_vectors(vectors, biases):
    mesh_dp, mesh_tensor = lax.axis_size("dp"), lax.axis_size("tensor")
    parts = [part.reshape(mesh_dp, mesh_tensor, -1) for part in vectors]
    packed = jnp.concatenate(parts, axis=2)
    width = packed.shape[2]
    rows = [packed.reshape(mesh_dp, -1)] + [part.reshape(mesh_dp, -1) for part in biases]
    mine = lax.psum_scatter(jnp.concatenate(rows, axis=1), "dp", scatter_dimension=0, tiled=True)[0]
    own = lax.psum_scatter(
        mine[: mesh_tensor * width].reshape(mesh_tensor, width),
        "tensor",
        scatter_dimension=0,
        tiled=True,
    )[0]
    sent = list(own.reshape(len(vectors), -1))
    start = mesh_tensor * width
    for part in biases:
        size = part.shape[0] // mesh_dp
        sent.append(mine[start : start + size])
        start += size
    return sent


def attn_fwd_kernel(len_ref, q_ref, k_ref, v_ref, ctx_ref, p_ref):
    seq_len = q_ref.shape[0]
    rows = min(256, seq_len)
    length = len_ref[pl.program_id(0)]
    spot = lax.broadcasted_iota(jnp.int32, (1, seq_len), 1)
    bias = jnp.where(spot < length, 0.0, -jnp.inf).astype(jnp.float32)
    scale = HEAD_DIM ** (-0.5)

    def step(i, carry):
        here = pl.ds(pl.multiple_of(i * rows, rows), rows)
        parts = []
        for h in range(2):
            cols = slice(h * HEAD_DIM, (h + 1) * HEAD_DIM)
            scores = dense_nt(q_ref[here, cols], k_ref[:, cols]) * scale + bias
            top = jnp.max(scores, axis=-1, keepdims=True)
            grown = jnp.exp(scores - top)
            total = jnp.sum(grown, axis=-1, keepdims=True)
            probs = (grown * (1.0 / total)).astype(jnp.bfloat16)
            p_ref[h, here, :] = probs
            parts.append(dense(probs, v_ref[:, cols]))
        ctx_ref[here, :] = jnp.concatenate(parts, axis=1).astype(jnp.bfloat16)
        return carry

    lax.fori_loop(0, seq_len // rows, step, 0)


def attention_fwd(q_rows, k_rows, v_rows, lengths):
    seqs = lengths.shape[0]
    seq_len = q_rows.shape[0] // seqs
    pairs = q_rows.shape[1] // (2 * HEAD_DIM)
    tile = pl.BlockSpec((seq_len, 2 * HEAD_DIM), lambda s, h, ln: (s, h))
    return pl.pallas_call(
        attn_fwd_kernel,
        grid_spec=pltpu.PrefetchScalarGridSpec(
            num_scalar_prefetch=1,
            grid=(seqs, pairs),
            in_specs=[tile, tile, tile],
            out_specs=[
                tile,
                pl.BlockSpec((2, seq_len, seq_len), lambda s, h, ln: (s * pairs + h, 0, 0)),
            ],
        ),
        out_shape=[
            jax.ShapeDtypeStruct(q_rows.shape, jnp.bfloat16),
            jax.ShapeDtypeStruct((seqs * pairs * 2, seq_len, seq_len), jnp.bfloat16),
        ],
        compiler_params=pltpu.CompilerParams(vmem_limit_bytes=48 << 20),
        name="attn_fwd",
    )(lengths, q_rows, k_rows, v_rows)


def attn_bwd_kernel(q_ref, k_ref, v_ref, p_ref, g_ref, dq_ref, dk_ref, dv_ref, qb_ref, vb_ref, dk_sum, dv_sum):
    seq_len = q_ref.shape[0]
    rows = min(256, seq_len)
    scale = HEAD_DIM ** (-0.5)
    dk_sum[...] = jnp.zeros_like(dk_sum)
    dv_sum[...] = jnp.zeros_like(dv_sum)

    def step(i, total):
        here = pl.ds(pl.multiple_of(i * rows, rows), rows)
        parts = []
        for h in range(2):
            cols = slice(h * HEAD_DIM, (h + 1) * HEAD_DIM)
            grad = g_ref[here, cols]
            probs_b = p_ref[h, here, :]
            probs = probs_b.astype(jnp.float32)
            d_probs = dense_nt(grad, v_ref[:, cols])
            inner = jnp.sum(probs * d_probs, axis=-1, keepdims=True)
            d_scores = (probs * (d_probs - inner)).astype(jnp.bfloat16)
            parts.append(dense(d_scores, k_ref[:, cols]) * scale)
            dv_sum[cols, :] += dense_tn(grad, probs_b)
            dk_sum[cols, :] += dense_tn(q_ref[here, cols], d_scores)
        d_query = jnp.concatenate(parts, axis=1)
        dq_ref[here, :] = d_query.astype(jnp.bfloat16)
        return total + jnp.sum(d_query, axis=0, keepdims=True)

    qb_ref[0] = lax.fori_loop(0, seq_len // rows, step, jnp.zeros((1, 2 * HEAD_DIM), jnp.float32))
    dk_ref[...] = (jnp.transpose(dk_sum[...]) * scale).astype(jnp.bfloat16)
    d_value = jnp.transpose(dv_sum[...])
    dv_ref[...] = d_value.astype(jnp.bfloat16)
    vb_ref[0] = jnp.sum(d_value, axis=0, keepdims=True)


def attention_bwd(q_rows, k_rows, v_rows, probs_b, d_context, seqs):
    seq_len = q_rows.shape[0] // seqs
    wide = 2 * HEAD_DIM
    pairs = q_rows.shape[1] // wide
    tile = pl.BlockSpec((seq_len, wide), lambda s, h: (s, h))
    line = pl.BlockSpec((1, 1, wide), lambda s, h: (s, 0, h))
    grads = jax.ShapeDtypeStruct(q_rows.shape, jnp.bfloat16)
    sums = jax.ShapeDtypeStruct((seqs, 1, q_rows.shape[1]), jnp.float32)
    dq, dk, dv, qb, vb = pl.pallas_call(
        attn_bwd_kernel,
        grid=(seqs, pairs),
        in_specs=[
            tile,
            tile,
            tile,
            pl.BlockSpec((2, seq_len, seq_len), lambda s, h: (s * pairs + h, 0, 0)),
            tile,
        ],
        out_specs=[tile, tile, tile, line, line],
        out_shape=[grads, grads, grads, sums, sums],
        scratch_shapes=[
            pltpu.VMEM((wide, seq_len), jnp.float32),
            pltpu.VMEM((wide, seq_len), jnp.float32),
        ],
        compiler_params=pltpu.CompilerParams(vmem_limit_bytes=48 << 20),
        name="attn_bwd",
    )(q_rows, k_rows, v_rows, probs_b, d_context)
    return dq, dk, dv, jnp.sum(qb, axis=(0, 1)), jnp.sum(vb, axis=(0, 1))


def per_device(
    block_input,
    lengths,
    query_weight,
    key_weight,
    value_weight,
    query_bias,
    value_bias,
    output_weight,
    output_bias,
    first_gain,
    first_shift,
    inner_weight,
    inner_bias,
    outer_weight,
    outer_bias,
    second_gain,
    second_shift,
    cotangent,
):
    seq_rows = whole_rows(block_input)
    (
        full_obias,
        full_gain1,
        full_shift1,
        full_bias2,
        full_gain2,
        full_shift2,
        bias_query,
        bias_value,
        bias_inner,
    ) = gather_vectors(
        (output_bias, first_gain, first_shift, outer_bias, second_gain, second_shift),
        (query_bias, value_bias, inner_bias),
    )
    wide_query = lax.all_gather(query_weight, "dp", axis=0, tiled=True)
    wide_key = lax.all_gather(key_weight, "dp", axis=0, tiled=True)
    wide_value = lax.all_gather(value_weight, "dp", axis=0, tiled=True)
    wide_output = lax.all_gather(output_weight, "dp", axis=1, tiled=True)
    wide_inner = lax.all_gather(inner_weight, "dp", axis=0, tiled=True)
    wide_outer = lax.all_gather(outer_weight, "dp", axis=1, tiled=True)
    q_rows = (dense(seq_rows, wide_query) + bias_query).astype(jnp.bfloat16)
    k_rows = dense(seq_rows, wide_key).astype(jnp.bfloat16)
    v_rows = (dense(seq_rows, wide_value) + bias_value).astype(jnp.bfloat16)
    context, probs_b = attention_fwd(q_rows, k_rows, v_rows, lengths)
    own_context = lax.all_to_all(context, "tensor", split_axis=0, concat_axis=1, tiled=True)
    all_output = lax.all_gather(wide_output, "tensor", axis=0, tiled=True)
    attn_sum = dense(own_context, all_output)
    resid_one = block_input.astype(jnp.float32) + attn_sum + full_obias
    middle = row_norm(resid_one, full_gain1, full_shift1)
    middle_rows = whole_rows(middle.astype(jnp.bfloat16))
    pre_act = dense(middle_rows, wide_inner) + bias_inner
    hidden_b = (pre_act * gelu_cdf(pre_act)).astype(jnp.bfloat16)
    resid_two = middle + share_rows(dense(hidden_b, wide_outer)) + full_bias2
    block_output = row_norm(resid_two, full_gain2, full_shift2).astype(jnp.bfloat16)
    d_resid2, gain2_grad, shift2_grad = norm_back(
        resid_two, full_gain2, cotangent.astype(jnp.float32)
    )
    ffn_rows = whole_rows(d_resid2.astype(jnp.bfloat16))
    gelu_slope = gelu_cdf(pre_act) + pre_act * inv_root2pi * jnp.exp(-0.5 * pre_act * pre_act)
    d_pre = dense_nt(ffn_rows, wide_outer) * gelu_slope
    d_pre_b = d_pre.astype(jnp.bfloat16)
    ibias_grad = jnp.sum(d_pre, axis=0)
    d_middle = share_rows(dense_nt(d_pre_b, wide_inner)) + d_resid2
    sent_outer = share_grad(dense_tn(hidden_b, ffn_rows), 1)
    sent_inner = share_grad(dense_tn(middle_rows, d_pre_b), 0)
    d_resid1, gain1_grad, shift1_grad = norm_back(resid_one, full_gain1, d_middle)
    d_attn = d_resid1.astype(jnp.bfloat16)
    own_d_context = dense_nt(d_attn, all_output).astype(jnp.bfloat16)
    d_context = lax.all_to_all(own_d_context, "tensor", split_axis=1, concat_axis=0, tiled=True)
    attn_rows = whole_rows(d_attn)
    sent_output = share_grad(dense_tn(context, attn_rows), 1)
    dq_b, dk_b, dv_b, qbias_grad, vbias_grad = attention_bwd(
        q_rows, k_rows, v_rows, probs_b, d_context, lengths.shape[0]
    )
    input_grad = (
        share_rows(
            dense_nt(dq_b, wide_query) + dense_nt(dk_b, wide_key) + dense_nt(dv_b, wide_value)
        )
        + d_resid1
    )
    sent_query = share_grad(dense_tn(seq_rows, dq_b), 0)
    sent_key = share_grad(dense_tn(seq_rows, dk_b), 0)
    sent_value = share_grad(dense_tn(seq_rows, dv_b), 0)
    (
        sent_obias,
        sent_gain1,
        sent_shift1,
        sent_bias2,
        sent_gain2,
        sent_shift2,
        sent_qbias,
        sent_vbias,
        sent_ibias,
    ) = share_vectors(
        (
            jnp.sum(d_resid1, axis=0),
            gain1_grad,
            shift1_grad,
            jnp.sum(d_resid2, axis=0),
            gain2_grad,
            shift2_grad,
        ),
        (qbias_grad, vbias_grad, ibias_grad),
    )
    return (
        block_output,
        input_grad,
        sent_query,
        sent_key,
        sent_value,
        sent_qbias,
        sent_vbias,
        sent_output,
        sent_obias,
        sent_gain1,
        sent_shift1,
        sent_inner,
        sent_ibias,
        sent_outer,
        sent_bias2,
        sent_gain2,
        sent_shift2,
    )


def solution(mesh):
    return jax.shard_map(
        per_device,
        mesh=mesh,
        in_specs=(
            P(("dp", "tensor"), None),
            P("dp"),
            P("dp", "tensor"),
            P("dp", "tensor"),
            P("dp", "tensor"),
            P(("tensor", "dp")),
            P(("tensor", "dp")),
            P("tensor", "dp"),
            P(("dp", "tensor")),
            P(("dp", "tensor")),
            P(("dp", "tensor")),
            P("dp", "tensor"),
            P(("tensor", "dp")),
            P("tensor", "dp"),
            P(("dp", "tensor")),
            P(("dp", "tensor")),
            P(("dp", "tensor")),
            P(("dp", "tensor"), None),
        ),
        out_specs=(
            P(("dp", "tensor"), None),
            P(("dp", "tensor"), None),
            P("dp", "tensor"),
            P("dp", "tensor"),
            P("dp", "tensor"),
            P(("tensor", "dp")),
            P(("tensor", "dp")),
            P("tensor", "dp"),
            P(("dp", "tensor")),
            P(("dp", "tensor")),
            P(("dp", "tensor")),
            P("dp", "tensor"),
            P(("tensor", "dp")),
            P("tensor", "dp"),
            P(("dp", "tensor")),
            P(("dp", "tensor")),
            P(("dp", "tensor")),
        ),
        check_vma=False,
    )
```
